32 devices in a mesh: group: 2 (over x), blk: 16 (over z, y, core).
Axes of the slice: x: 2, y: 2, z: 4, core: 2. Of those that a mesh axis runs over, the one named last changes fastest.
Arguments:
- tensors: bfloat16 [64, 256, 4, 256], P(('group', 'blk')), parts along dimension 0, may hold values from -6 to 6
- gate_terms: float32 [2, 16, 16], replicated, may hold values from -1.2 to 1.2
- right_proj: bfloat16 [32, 1024, 256], P('blk')
- left_proj: bfloat16 [32, 256, 1024], P('blk'), may hold values from -0.1875 to 0.1875
Outputs:
- evolved: bfloat16 [64, 256, 4, 256], P(('group', 'blk')), parts along dimension 0
- records: float32 [8, 2], P('group'), parts along dimension 0
The draws below stay inside these ranges and needn't reach their ends.
There are 2 independent parts, one for each index of `group`. The reference program is written for one: setup_inputs(seed, part) draws one part's arguments, and reference() takes and returns one part's arrays. A program takes and returns all parts, laid end to end along the dimension named above; an argument that names none is the same for every part. Nothing has to cross between parts.
All inputs are finite; a program needn't handle non-finite values.
Results may differ from the reference program's by a relative error of at most 0.024.
Values may be sent and summed in bfloat16 or wider, within the bound.
A program may use at most 64 MiB of HBM per device.

```python
import math
import jax
import jax.numpy as jnp
from jax import lax

CHI = 256
D = 4
LAYERS = 4
SITES = 32
BONDS = 32


def draw_right_proj(key, part):
    base = jax.random.normal(key, (BONDS, D * CHI, CHI), jnp.float32) / math.sqrt(D * CHI)
    ramp = 1.0 + 0.05 * jnp.arange(BONDS, dtype=jnp.float32) / (BONDS - 1)
    return (base * ramp[:, None, None]).astype(jnp.bfloat16)


def block_levels(own_key, dims, shards, low, high):
    gain = 1.0
    for position, shards_of in shards:
        heights = jax.random.uniform(jax.random.fold_in(jax.random.fold_in(own_key, 6), position), (shards_of,), jnp.float32, low / len(shards), high / len(shards))
        gain = gain * jnp.repeat(jnp.exp(heights), dims[position] // shards_of).reshape((-1,) + (1,) * (len(dims) - 1 - position))
    return gain


def centred(own_key, extent, scale, limit, split=(), held_as=jnp.bfloat16):
    values = scale * jax.random.normal(own_key, extent, jnp.float32)
    if split:
        values = values * block_levels(own_key, extent, split, -0.22, 0.18)
    return jnp.clip(values, -limit, limit).astype(held_as)


def setup_inputs(seed: int = 0, part: int = 0) -> dict:
    key_of = jax.random.split(jax.random.key(seed), 5)
    part_keys = jax.random.split(jax.random.fold_in(key_of[4], part), 5)
    tensors = centred(part_keys[0], (SITES, CHI, D, CHI), 1.0, 6.0, ((0, 16),))
    gate_terms = centred(key_of[1], (2, D * D, D * D), 0.3, 1.2, (), jnp.float32)
    right_proj = draw_right_proj(jax.random.fold_in(key_of[4], 71), part)
    left_proj = centred(key_of[3], (BONDS, CHI, CHI * D), (CHI * D) ** -0.5, 0.1875, ((0, 16),))
    return {"tensors": tensors, "gate_terms": gate_terms, "right_proj": right_proj, "left_proj": left_proj}


def bond_update(left_site, right_site, gate_table, rproj_one, lproj_one):
    theta = jnp.dot(left_site.reshape(CHI * D, CHI), right_site.reshape(CHI, D * CHI), preferred_element_type=jnp.float32)
    theta_four = theta.reshape(CHI, D, D, CHI)
    gated = jnp.einsum('stuv,auvc->astc', gate_table, theta_four, precision=lax.Precision.HIGHEST)
    gated = gated.reshape(CHI * D, D * CHI).astype(jnp.bfloat16)
    fresh_left = jnp.dot(gated, rproj_one, preferred_element_type=jnp.float32)
    fresh_right = jnp.dot(lproj_one, gated, preferred_element_type=jnp.float32)
    return (fresh_left.reshape(CHI, D, CHI), fresh_right.reshape(CHI, D, CHI))

def reference(tensors, gate_terms, right_proj, left_proj):
    identity_matrix = jnp.eye(D * D, dtype=jnp.float32)
    entry_count = float(SITES * CHI * D * CHI)
    current = tensors
    rows_out = []
    for layer_index in range(LAYERS):
        parity = layer_index % 2
        gate_table = (identity_matrix + gate_terms[parity]).reshape(D, D, D, D)
        if parity == 0:
            lefts = current[0::2]
            rights = current[1::2]
        else:
            lefts = current[1::2]
            rights = jnp.roll(current, -1, axis=0)[1::2]

        def apply_pair(item):
            return bond_update(item[0], item[1], gate_table, item[2], item[3])
        fresh_left, fresh_right = lax.map(apply_pair, (lefts, rights, right_proj[parity::2], left_proj[parity::2]))
        updated = jnp.stack([fresh_left, fresh_right], axis=1).reshape(SITES, CHI, D, CHI)
        if parity == 1:
            updated = jnp.roll(updated, 1, axis=0)
        square_sum = jnp.sum(updated * updated)
        largest = jnp.max(jnp.abs(updated))
        root_mean = jnp.sqrt(square_sum / entry_count + 1e-06)
        rows_out.append(jnp.stack([jnp.log(root_mean), jnp.log(largest / root_mean)]))
        current = (updated / root_mean).astype(jnp.bfloat16)
    return (current, jnp.stack(rows_out))
```

```python
import functools
import jax
import jax.numpy as jnp
from jax import lax
from jax.experimental import pallas as pl
from jax.experimental.pallas import tpu as pltpu
from jax.sharding import PartitionSpec as P

LAYERS = 4
HALF = 128
GROUP = 16


def mm(a, b):
    return jnp.dot(a, b, preferred_element_type=jnp.float32)


def sweep_kernel(n, chi, d, entries, x_ref, w_ref, rp_ref, lp_ref, out_ref, rec_ref,
                 site_a, site_b, ahead, back, r_in, a_in, gated, lp_perm, acc, mine, seen,
                 fs, fr, bs, br, ss, sr):
    me = lax.axis_index("blk")
    right, left = lax.rem(me + 1, n), lax.rem(me + n - 1, n)
    quarter = chi // d
    barrier = pltpu.get_barrier_semaphore()

    def greet(k, carry):
        pl.semaphore_signal(barrier, inc=1, device_id={"blk": lax.rem(me + k, n)},
                            device_id_type=pl.DeviceIdType.MESH)
        return carry

    lax.fori_loop(1, n, greet, 0)

    rows = lax.broadcasted_iota(jnp.int32, (chi, chi), 0)
    cols = lax.broadcasted_iota(jnp.int32, (chi, chi), 1)
    to_block = jnp.where((rows // quarter == cols % d) & (rows % quarter == cols // d), 1.0, 0.0).astype(jnp.bfloat16)
    to_plain = jnp.where((cols // quarter == rows % d) & (cols % quarter == rows // d), 1.0, 0.0).astype(jnp.bfloat16)
    wide = d * HALF
    wrow = lax.broadcasted_iota(jnp.int32, (wide, wide), 0)
    wcol = lax.broadcasted_iota(jnp.int32, (wide, wide), 1)
    spread = jnp.where((wcol // HALF == wrow % d) & (wcol % HALF == wrow // d), 1.0, 0.0).astype(jnp.bfloat16)

    for which, site in ((0, site_a), (1, site_b)):
        def load(k, carry, which=which, site=site):
            block = mm(to_block, x_ref[which, pl.ds(k * chi, chi), :]).astype(jnp.bfloat16)
            for p in range(d):
                for h in range(2):
                    site[h, pl.ds(p * chi + k * quarter, quarter), :] = block[p * quarter:(p + 1) * quarter, h * HALF:(h + 1) * HALF]
            return carry
        lax.fori_loop(0, d, load, 0)
    for parity in range(2):
        for k in range(2):
            part = mm(lp_ref[parity, :, k * wide:(k + 1) * wide], spread).astype(jnp.bfloat16)
            for s in range(d):
                lp_perm[parity, :, s * chi + k * HALF:s * chi + (k + 1) * HALF] = part[:, s * HALF:(s + 1) * HALF]

    def theta_gate(h, parity, lhs_ref, rhs_ref):
        def tile(at, carry):
            lhs = jnp.concatenate([
                jnp.concatenate([lhs_ref[q, pl.ds(u * chi + at * quarter, quarter), :] for q in range(2)], axis=1)
                for u in range(d)], axis=0)
            rhs = jnp.concatenate([rhs_ref[h, v * chi:(v + 1) * chi, :] for v in range(d)], axis=1)
            th = mm(lhs, rhs).astype(jnp.bfloat16)
            for pair in range(quarter // GROUP // 2):
                stack = jnp.concatenate([
                    jnp.concatenate([
                        th[u * quarter + (2 * pair + j) * GROUP:u * quarter + (2 * pair + j + 1) * GROUP, v * HALF:(v + 1) * HALF]
                        for v in range(d) for u in range(d)], axis=0)
                    for j in range(2)], axis=1)
                mixed = mm(w_ref[parity], stack)
                mixed = (mixed[:chi] + mixed[chi:]).astype(jnp.bfloat16)
                for j in range(2):
                    for t in range(d):
                        for s in range(d):
                            top = (t * d + s) * GROUP
                            gated[h, pl.ds(s * chi + at * quarter + (2 * pair + j) * GROUP, GROUP), t * HALF:(t + 1) * HALF] = (
                                mixed[top:top + GROUP, j * HALF:(j + 1) * HALF])
            return carry
        lax.fori_loop(0, d, tile, 0)

    def note(value):
        folded = value.reshape(value.shape[0] // 8, 8, value.shape[1])
        sq = jnp.sum(folded * folded, axis=0)
        mx = jnp.max(jnp.abs(folded), axis=0)
        for c in range(value.shape[1] // HALF):
            acc[0] += sq[:, c * HALF:(c + 1) * HALF]
            acc[1] = jnp.maximum(acc[1], mx[:, c * HALF:(c + 1) * HALF])

    def new_right(h, parity, dst, scale):
        value = mm(lp_perm[parity], gated[h])
        if scale is not None:
            value = value * scale
        note(value)
        value = value.astype(jnp.bfloat16)
        for t in range(d):
            dst[h, t * chi:(t + 1) * chi, :] = value[:, t * HALF:(t + 1) * HALF]

    def new_left(parity, dst, scale):
        def tile(s, carry):
            here = pl.ds(s * chi, chi)
            lhs = jnp.concatenate([gated[0, here, :], gated[1, here, :]], axis=1)
            rhs = jnp.concatenate([rp_ref[parity, t * chi + h * HALF:t * chi + (h + 1) * HALF, :]
                                   for h in range(2) for t in range(d)], axis=0)
            value = mm(lhs, rhs)
            if scale is not None:
                value = value * scale
            note(value)
            value = value.astype(jnp.bfloat16)
            for h in range(2):
                dst[h, here, :] = value[:, h * HALF:(h + 1) * HALF]
            return carry
        lax.fori_loop(0, d, tile, 0)

    def forward(k, h):
        return pltpu.make_async_remote_copy(
            src_ref=ahead.at[k, h], dst_ref=r_in.at[k, h], send_sem=fs.at[k, h], recv_sem=fr.at[k, h],
            device_id={"blk": left}, device_id_type=pl.DeviceIdType.MESH)

    def backward(k, h):
        return pltpu.make_async_remote_copy(
            src_ref=back.at[k, h], dst_ref=a_in.at[k, h], send_sem=bs.at[k, h], recv_sem=br.at[k, h],
            device_id={"blk": right}, device_id_type=pl.DeviceIdType.MESH)

    def everyone(layer):
        return pltpu.make_async_remote_copy(
            src_ref=seen.at[layer], dst_ref=seen.at[layer], send_sem=ss.at[layer], recv_sem=sr.at[layer],
            device_id={"blk": right}, device_id_type=pl.DeviceIdType.MESH)

    def share(layer):
        mine[layer, 0:1, :] = jnp.sum(acc[0], axis=0, keepdims=True)
        mine[layer, 1:2, :] = jnp.max(acc[1], axis=0, keepdims=True)

        def send(k, carry):
            pltpu.make_async_remote_copy(
                src_ref=mine.at[layer], dst_ref=seen.at[layer, k - 1], send_sem=ss.at[layer], recv_sem=sr.at[layer],
                device_id={"blk": lax.rem(me + k, n)}, device_id_type=pl.DeviceIdType.MESH).start()
            return carry
        lax.fori_loop(1, n, send, 0)
        acc[...] = jnp.zeros_like(acc)

    def learn(layer):
        everyone(layer).wait_recv()
        got = seen[layer]
        own = mine[layer]
        squares = jnp.sum(jnp.sum(got, axis=0)[0:1] + own[0:1], axis=1, keepdims=True)
        largest = jnp.max(jnp.maximum(jnp.max(got, axis=0)[1:2], own[1:2]), axis=1, keepdims=True)
        power = squares / entries + 1e-06
        root = jnp.sqrt(power)
        lane = lax.broadcasted_iota(jnp.int32, (1, HALF), 1)
        rec_ref[layer:layer + 1, :] = jnp.where(lane == 0, jnp.log(root), jnp.log(largest / root))
        return power, root

    acc[...] = jnp.zeros_like(acc)
    scale, root = None, None
    for layer in range(LAYERS):
        parity, k = layer % 2, layer // 2
        if parity == 0:
            lhs = site_a
            if k > 0:
                lhs = a_in.at[k - 1]
                for h in range(2):
                    backward(k - 1, h).wait_recv()
            for h in range(2):
                theta_gate(h, parity, lhs, site_b)
            if layer > 0:
                power, root = learn(layer - 1)
                scale = 1.0 / power
            new_left(parity, ahead.at[k], scale)
            if layer == 0:
                pl.semaphore_wait(barrier, n - 1)
            for h in range(2):
                forward(k, h).start()
            for h in range(2):
                new_right(h, parity, site_b, scale)
        else:
            for h in range(2):
                forward(k, h).wait_recv()
                theta_gate(h, parity, site_b, r_in.at[k])
                if h == 0:
                    power, root = learn(layer - 1)
                    scale = 1.0 / power
                new_right(h, parity, back.at[k], scale)
                backward(k, h).start()
            new_left(parity, site_b, scale)
        share(layer)

    last = LAYERS // 2 - 1
    for h in range(2):
        backward(last, h).wait_recv()
    power, root = learn(LAYERS - 1)
    shrink = 1.0 / root
    for which, site in ((0, a_in.at[last]), (1, site_b)):
        def store(kk, carry, which=which, site=site):
            block = jnp.concatenate([
                jnp.concatenate([site[h, pl.ds(p * chi + kk * quarter, quarter), :] for h in range(2)], axis=1)
                for p in range(d)], axis=0)
            out_ref[which, pl.ds(kk * chi, chi), :] = (mm(to_plain, block) * shrink).astype(jnp.bfloat16)
            return carry
        lax.fori_loop(0, d, store, 0)
    for k in range(LAYERS // 2):
        for h in range(2):
            forward(k, h).wait_send()
            backward(k, h).wait_send()
    for layer in range(LAYERS):
        everyone(layer).wait_send()


def local(tensors, gate_terms, right_proj, left_proj):
    slots, chi, d, _ = tensors.shape
    n = lax.axis_size("blk")
    entries = float(n * slots * chi * d * chi)
    table = jnp.eye(d * d, dtype=jnp.float32)[None] + gate_terms
    table = table.reshape(2, d, d, d, d).transpose(0, 2, 1, 4, 3).reshape(2, d * d, d * d)
    high = lax.reduce_precision(table, 8, 7)
    both = jnp.concatenate([high, table - high], axis=1)
    eye = jnp.eye(GROUP, dtype=jnp.float32)
    mixer = (both[:, :, None, :, None] * eye[None, None, :, None, :]).reshape(2, 2 * d * d * GROUP, d * d * GROUP)
    mixer = mixer.astype(jnp.bfloat16)
    vmem = pl.BlockSpec(memory_space=pltpu.VMEM)
    half = (2, d * chi, HALF)
    dma = pltpu.SemaphoreType.DMA
    pairs = LAYERS // 2
    evolved, records = pl.pallas_call(
        functools.partial(sweep_kernel, n, chi, d, entries),
        out_shape=(jax.ShapeDtypeStruct((2, chi * d, chi), jnp.bfloat16),
                   jax.ShapeDtypeStruct((8, HALF), jnp.float32)),
        in_specs=[vmem] * 4,
        out_specs=(vmem, vmem),
        scratch_shapes=[
            pltpu.VMEM(half, jnp.bfloat16),
            pltpu.VMEM(half, jnp.bfloat16),
            pltpu.VMEM((pairs,) + half, jnp.bfloat16),
            pltpu.VMEM((pairs,) + half, jnp.bfloat16),
            pltpu.VMEM((pairs,) + half, jnp.bfloat16),
            pltpu.VMEM((pairs,) + half, jnp.bfloat16),
            pltpu.VMEM((2, d * chi, d * HALF), jnp.bfloat16),
            pltpu.VMEM((2, chi, d * chi), jnp.bfloat16),
            pltpu.VMEM((2, 8, HALF), jnp.float32),
            pltpu.VMEM((LAYERS, 2, HALF), jnp.float32),
            pltpu.VMEM((LAYERS, n - 1, 2, HALF), jnp.float32),
            dma((pairs, 2)), dma((pairs, 2)), dma((pairs, 2)), dma((pairs, 2)),
            dma((LAYERS,)), dma((LAYERS,)),
        ],
        compiler_params=pltpu.CompilerParams(collective_id=0, has_side_effects=True,
                                             vmem_limit_bytes=56 * 1024 * 1024),
        name="sweep",
    )(tensors.reshape(slots, chi * d, chi), mixer, right_proj, left_proj)
    return evolved.reshape(tensors.shape), records[:LAYERS, :2]


def solution(mesh):
    in_specs = (
        P(("group", "blk"), None, None, None),
        P(),
        P("blk", None, None),
        P("blk", None, None),
    )
    out_specs = (P(("group", "blk"), None, None, None), P("group", None))
    return jax.shard_map(local, mesh=mesh, in_specs=in_specs, out_specs=out_specs, check_vma=False)
```

```python
import functools
import jax
import jax.numpy as jnp
from jax import lax
from jax.experimental import pallas as pl
from jax.experimental.pallas import tpu as pltpu
from jax.sharding import PartitionSpec as P

LAYERS = 4
HALF = 128
GROUP = 16


def mm(a, b):
    return jnp.dot(a, b, preferred_element_type=jnp.float32)


def sweep_kernel(n, chi, d, entries, x_ref, gate_ref, rp_ref, lp_ref, out_ref, rec_ref,
                 w_ref, site_a, site_b, ahead, back, r_in, a_in, gated, lp_perm, acc, mine, seen,
                 fs, fr, bs, br, ss, sr):
    me = lax.axis_index("blk")
    right, left = lax.rem(me + 1, n), lax.rem(me + n - 1, n)
    quarter = chi // d
    barrier = pltpu.get_barrier_semaphore()

    def greet(k, carry):
        pl.semaphore_signal(barrier, inc=1, device_id={"blk": lax.rem(me + k, n)},
                            device_id_type=pl.DeviceIdType.MESH)
        return carry

    lax.fori_loop(1, n, greet, 0)

    rows = lax.broadcasted_iota(jnp.int32, (chi, chi), 0)
    cols = lax.broadcasted_iota(jnp.int32, (chi, chi), 1)
    to_block = jnp.where((rows // quarter == cols % d) & (rows % quarter == cols // d), 1.0, 0.0).astype(jnp.bfloat16)
    to_plain = jnp.where((cols // quarter == rows % d) & (cols % quarter == rows // d), 1.0, 0.0).astype(jnp.bfloat16)
    wide = d * HALF
    wrow = lax.broadcasted_iota(jnp.int32, (wide, wide), 0)
    wcol = lax.broadcasted_iota(jnp.int32, (wide, wide), 1)
    spread = jnp.where((wcol // HALF == wrow % d) & (wcol % HALF == wrow // d), 1.0, 0.0).astype(jnp.bfloat16)

    pairs = d * d
    pick_row = lax.broadcasted_iota(jnp.int32, (chi, pairs), 0) // GROUP
    pick_from = lax.broadcasted_iota(jnp.int32, (chi, pairs), 1)
    pick_left = jnp.where(pick_from == (pick_row % d) * d + pick_row // d, 1.0, 0.0).astype(jnp.bfloat16)
    pick_col = lax.broadcasted_iota(jnp.int32, (pairs, chi), 1) // GROUP
    pick_into = lax.broadcasted_iota(jnp.int32, (pairs, chi), 0)
    pick_right = jnp.where(pick_into == (pick_col % d) * d + pick_col // d, 1.0, 0.0).astype(jnp.bfloat16)
    same = rows % GROUP == cols % GROUP
    unit = jnp.where(lax.broadcasted_iota(jnp.int32, (pairs, pairs), 0)
                     == lax.broadcasted_iota(jnp.int32, (pairs, pairs), 1), 1.0, 0.0)

    def mixer(parity):
        table = unit + gate_ref[parity]
        high = table.astype(jnp.bfloat16)
        low = (table - high.astype(jnp.float32)).astype(jnp.bfloat16)
        for position, term in ((0, high), (1, low)):
            spread_rows = mm(pick_left, term).astype(jnp.bfloat16)
            full = jnp.where(same, mm(spread_rows, pick_right), 0.0)
            w_ref[parity, position * chi:(position + 1) * chi, :] = full.astype(jnp.bfloat16)

    mixer(0)
    mixer(1)

    for which, site in ((0, site_a), (1, site_b)):
        def load(k, carry, which=which, site=site):
            block = mm(to_block, x_ref[which, pl.ds(k * quarter, quarter)].reshape(chi, chi)).astype(jnp.bfloat16)
            for p in range(d):
                for h in range(2):
                    site[h, pl.ds(p * chi + k * quarter, quarter), :] = block[p * quarter:(p + 1) * quarter, h * HALF:(h + 1) * HALF]
            return carry
        lax.fori_loop(0, d, load, 0)
    for parity in range(2):
        for k in range(2):
            part = mm(lp_ref[parity, :, k * wide:(k + 1) * wide], spread).astype(jnp.bfloat16)
            for s in range(d):
                lp_perm[parity, :, s * chi + k * HALF:s * chi + (k + 1) * HALF] = part[:, s * HALF:(s + 1) * HALF]

    def theta_gate(h, parity, lhs_ref, rhs_ref):
        def tile(at, carry):
            lhs = jnp.concatenate([
                jnp.concatenate([lhs_ref[q, pl.ds(u * chi + at * quarter, quarter), :] for q in range(2)], axis=1)
                for u in range(d)], axis=0)
            rhs = jnp.concatenate([rhs_ref[h, v * chi:(v + 1) * chi, :] for v in range(d)], axis=1)
            th = mm(lhs, rhs).astype(jnp.bfloat16)
            for pair in range(quarter // GROUP // 2):
                stack = jnp.concatenate([
                    jnp.concatenate([
                        th[u * quarter + (2 * pair + j) * GROUP:u * quarter + (2 * pair + j + 1) * GROUP, v * HALF:(v + 1) * HALF]
                        for v in range(d) for u in range(d)], axis=0)
                    for j in range(2)], axis=1)
                mixed = mm(w_ref[parity], stack)
                mixed = (mixed[:chi] + mixed[chi:]).astype(jnp.bfloat16)
                for j in range(2):
                    for t in range(d):
                        for s in range(d):
                            top = (t * d + s) * GROUP
                            gated[h, pl.ds(s * chi + at * quarter + (2 * pair + j) * GROUP, GROUP), t * HALF:(t + 1) * HALF] = (
                                mixed[top:top + GROUP, j * HALF:(j + 1) * HALF])
            return carry
        lax.fori_loop(0, d, tile, 0)

    def note(value):
        folded = value.reshape(value.shape[0] // 8, 8, value.shape[1])
        sq = jnp.sum(folded * folded, axis=0)
        mx = jnp.max(jnp.abs(folded), axis=0)
        for c in range(value.shape[1] // HALF):
            acc[0] += sq[:, c * HALF:(c + 1) * HALF]
            acc[1] = jnp.maximum(acc[1], mx[:, c * HALF:(c + 1) * HALF])

    def new_right(h, parity, dst, scale):
        value = mm(lp_perm[parity], gated[h])
        if scale is not None:
            value = value * scale
        note(value)
        value = value.astype(jnp.bfloat16)
        for t in range(d):
            dst[h, t * chi:(t + 1) * chi, :] = value[:, t * HALF:(t + 1) * HALF]

    def new_left(parity, dst, scale):
        def tile(s, carry):
            here = pl.ds(s * chi, chi)
            lhs = jnp.concatenate([gated[0, here, :], gated[1, here, :]], axis=1)
            rhs = jnp.concatenate([rp_ref[parity, t * chi + h * HALF:t * chi + (h + 1) * HALF, :]
                                   for h in range(2) for t in range(d)], axis=0)
            value = mm(lhs, rhs)
            if scale is not None:
                value = value * scale
            note(value)
            value = value.astype(jnp.bfloat16)
            for h in range(2):
                dst[h, here, :] = value[:, h * HALF:(h + 1) * HALF]
            return carry
        lax.fori_loop(0, d, tile, 0)

    def forward(k, h):
        return pltpu.make_async_remote_copy(
            src_ref=ahead.at[k, h], dst_ref=r_in.at[k, h], send_sem=fs.at[k, h], recv_sem=fr.at[k, h],
            device_id={"blk": left}, device_id_type=pl.DeviceIdType.MESH)

    def backward(k, h):
        return pltpu.make_async_remote_copy(
            src_ref=back.at[k, h], dst_ref=a_in.at[k, h], send_sem=bs.at[k, h], recv_sem=br.at[k, h],
            device_id={"blk": right}, device_id_type=pl.DeviceIdType.MESH)

    def everyone(layer):
        return pltpu.make_async_remote_copy(
            src_ref=seen.at[layer], dst_ref=seen.at[layer], send_sem=ss.at[layer], recv_sem=sr.at[layer],
            device_id={"blk": right}, device_id_type=pl.DeviceIdType.MESH)

    def share(layer):
        mine[layer, 0:1, :] = jnp.sum(acc[0], axis=0, keepdims=True)
        mine[layer, 1:2, :] = jnp.max(acc[1], axis=0, keepdims=True)

        def send(k, carry):
            pltpu.make_async_remote_copy(
                src_ref=mine.at[layer], dst_ref=seen.at[layer, k - 1], send_sem=ss.at[layer], recv_sem=sr.at[layer],
                device_id={"blk": lax.rem(me + k, n)}, device_id_type=pl.DeviceIdType.MESH).start()
            return carry
        lax.fori_loop(1, n, send, 0)
        acc[...] = jnp.zeros_like(acc)

    def learn(layer):
        everyone(layer).wait_recv()
        got = seen[layer]
        own = mine[layer]
        squares = jnp.sum(jnp.sum(got, axis=0)[0:1] + own[0:1], axis=1, keepdims=True)
        largest = jnp.max(jnp.maximum(jnp.max(got, axis=0)[1:2], own[1:2]), axis=1, keepdims=True)
        power = squares / entries + 1e-06
        root = jnp.sqrt(power)
        lane = lax.broadcasted_iota(jnp.int32, (1, 2), 1)
        rec_ref[layer:layer + 1, :] = jnp.where(lane == 0, jnp.log(root), jnp.log(largest / root))
        return power, root

    acc[...] = jnp.zeros_like(acc)
    scale, root = None, None
    for layer in range(LAYERS):
        parity, k = layer % 2, layer // 2
        if parity == 0:
            lhs = site_a
            if k > 0:
                lhs = a_in.at[k - 1]
                for h in range(2):
                    backward(k - 1, h).wait_recv()
            for h in range(2):
                theta_gate(h, parity, lhs, site_b)
            if layer > 0:
                power, root = learn(layer - 1)
                scale = 1.0 / power
            new_left(parity, ahead.at[k], scale)
            if layer == 0:
                pl.semaphore_wait(barrier, n - 1)
            for h in range(2):
                forward(k, h).start()
            for h in range(2):
                new_right(h, parity, site_b, scale)
        else:
            for h in range(2):
                forward(k, h).wait_recv()
                theta_gate(h, parity, site_b, r_in.at[k])
                if h == 0:
                    power, root = learn(layer - 1)
                    scale = 1.0 / power
                new_right(h, parity, back.at[k], scale)
                backward(k, h).start()
            new_left(parity, site_b, scale)
        share(layer)

    last = LAYERS // 2 - 1
    for h in range(2):
        backward(last, h).wait_recv()
    power, root = learn(LAYERS - 1)
    shrink = 1.0 / root
    for which, site in ((0, a_in.at[last]), (1, site_b)):
        def store(kk, carry, which=which, site=site):
            block = jnp.concatenate([
                jnp.concatenate([site[h, pl.ds(p * chi + kk * quarter, quarter), :] for h in range(2)], axis=1)
                for p in range(d)], axis=0)
            out_ref[which, pl.ds(kk * quarter, quarter)] = (mm(to_plain, block) * shrink).astype(jnp.bfloat16).reshape(quarter, d, chi)
            return carry
        lax.fori_loop(0, d, store, 0)
    for k in range(LAYERS // 2):
        for h in range(2):
            forward(k, h).wait_send()
            backward(k, h).wait_send()
    for layer in range(LAYERS):
        everyone(layer).wait_send()


def local(tensors, gate_terms, right_proj, left_proj):
    slots, chi, d, _ = tensors.shape
    n = lax.axis_size("blk")
    entries = float(n * slots * chi * d * chi)
    vmem = pl.BlockSpec(memory_space=pltpu.VMEM)
    half = (2, d * chi, HALF)
    dma = pltpu.SemaphoreType.DMA
    pairs = LAYERS // 2
    evolved, records = pl.pallas_call(
        functools.partial(sweep_kernel, n, chi, d, entries),
        out_shape=(jax.ShapeDtypeStruct(tensors.shape, jnp.bfloat16),
                   jax.ShapeDtypeStruct((LAYERS, 2), jnp.float32)),
        in_specs=[vmem] * 4,
        out_specs=(vmem, vmem),
        scratch_shapes=[
            pltpu.VMEM((2, 2 * d * d * GROUP, d * d * GROUP), jnp.bfloat16),
            pltpu.VMEM(half, jnp.bfloat16),
            pltpu.VMEM(half, jnp.bfloat16),
            pltpu.VMEM((pairs,) + half, jnp.bfloat16),
            pltpu.VMEM((pairs,) + half, jnp.bfloat16),
            pltpu.VMEM((pairs,) + half, jnp.bfloat16),
            pltpu.VMEM((pairs,) + half, jnp.bfloat16),
            pltpu.VMEM((2, d * chi, d * HALF), jnp.bfloat16),
            pltpu.VMEM((2, chi, d * chi), jnp.bfloat16),
            pltpu.VMEM((2, 8, HALF), jnp.float32),
            pltpu.VMEM((LAYERS, 2, HALF), jnp.float32),
            pltpu.VMEM((LAYERS, n - 1, 2, HALF), jnp.float32),
            dma((pairs, 2)), dma((pairs, 2)), dma((pairs, 2)), dma((pairs, 2)),
            dma((LAYERS,)), dma((LAYERS,)),
        ],
        compiler_params=pltpu.CompilerParams(collective_id=0, has_side_effects=True,
                                             vmem_limit_bytes=56 * 1024 * 1024),
        name="sweep",
    )(tensors, gate_terms, right_proj, left_proj)
    return evolved, records


def solution(mesh):
    in_specs = (
        P(("group", "blk"), None, None, None),
        P(),
        P("blk", None, None),
        P("blk", None, None),
    )
    out_specs = (P(("group", "blk"), None, None, None), P("group", None))
    return jax.shard_map(local, mesh=mesh, in_specs=in_specs, out_specs=out_specs, check_vma=False)
```

```python
import functools
import jax
import jax.numpy as jnp
from jax import lax
from jax.experimental import pallas as pl
from jax.experimental.pallas import tpu as pltpu
from jax.sharding import PartitionSpec as P

LAYERS = 4
HALF = 128
GROUP = 16
UNROLL = 4


def mm(a, b):
    return jnp.dot(a, b, preferred_element_type=jnp.float32)


def sweep_kernel(n, chi, d, entries, x_hbm, gate_ref, rp_hbm, lp_hbm, out_ref, rec_ref,
                 x_ref, rp_ref, lp_ref, w_ref, site_a, site_b, ahead, back, r_in, a_in, gated, lp_perm, acc, mine, seen,
                 xs, ps, fs, fr, bs, br, ss, sr):
    me = lax.axis_index("blk")
    right, left = lax.rem(me + 1, n), lax.rem(me + n - 1, n)
    quarter = chi // d
    barrier = pltpu.get_barrier_semaphore()
    x_copies = [pltpu.make_async_copy(x_hbm.at[i], x_ref.at[i], xs.at[i]) for i in range(2)]
    rp_copies = [pltpu.make_async_copy(rp_hbm.at[i], rp_ref.at[i], ps.at[0, i]) for i in range(2)]
    lp_copies = [pltpu.make_async_copy(lp_hbm.at[i], lp_ref.at[i], ps.at[1, i]) for i in range(2)]
    for copy in x_copies + [rp_copies[0], lp_copies[0], lp_copies[1], rp_copies[1]]:
        copy.start()

    def greet(k, carry):
        pl.semaphore_signal(barrier, inc=1, device_id={"blk": lax.rem(me + k, n)},
                            device_id_type=pl.DeviceIdType.MESH)
        return carry

    lax.fori_loop(1, n, greet, 0)

    rows = lax.broadcasted_iota(jnp.int32, (chi, chi), 0)
    cols = lax.broadcasted_iota(jnp.int32, (chi, chi), 1)
    to_block = jnp.where((rows // quarter == cols % d) & (rows % quarter == cols // d), 1.0, 0.0).astype(jnp.bfloat16)
    to_plain = jnp.where((cols // quarter == rows % d) & (cols % quarter == rows // d), 1.0, 0.0).astype(jnp.bfloat16)
    wide = d * HALF
    wrow = lax.broadcasted_iota(jnp.int32, (wide, wide), 0)
    wcol = lax.broadcasted_iota(jnp.int32, (wide, wide), 1)
    spread = jnp.where((wcol // HALF == wrow % d) & (wcol % HALF == wrow // d), 1.0, 0.0).astype(jnp.bfloat16)

    pairs = d * d
    pick_row = lax.broadcasted_iota(jnp.int32, (chi, pairs), 0) // GROUP
    pick_from = lax.broadcasted_iota(jnp.int32, (chi, pairs), 1)
    pick_left = jnp.where(pick_from == (pick_row % d) * d + pick_row // d, 1.0, 0.0).astype(jnp.bfloat16)
    pick_col = lax.broadcasted_iota(jnp.int32, (pairs, chi), 1) // GROUP
    pick_into = lax.broadcasted_iota(jnp.int32, (pairs, chi), 0)
    pick_right = jnp.where(pick_into == (pick_col % d) * d + pick_col // d, 1.0, 0.0).astype(jnp.bfloat16)
    same = rows % GROUP == cols % GROUP
    unit = jnp.where(lax.broadcasted_iota(jnp.int32, (pairs, pairs), 0)
                     == lax.broadcasted_iota(jnp.int32, (pairs, pairs), 1), 1.0, 0.0)

    def mixer(parity):
        table = unit + gate_ref[parity]
        high = table.astype(jnp.bfloat16)
        low = (table - high.astype(jnp.float32)).astype(jnp.bfloat16)
        for position, term in ((0, high), (1, low)):
            spread_rows = mm(pick_left, term).astype(jnp.bfloat16)
            full = jnp.where(same, mm(spread_rows, pick_right), 0.0)
            w_ref[parity, position * chi:(position + 1) * chi, :] = full.astype(jnp.bfloat16)

    mixer(0)

    for which, site in ((0, site_a), (1, site_b)):
        x_copies[which].wait()

        def load(k, carry, which=which, site=site):
            block = mm(to_block, x_ref[which, pl.ds(k * quarter, quarter)].reshape(chi, chi)).astype(jnp.bfloat16)
            for p in range(d):
                for h in range(2):
                    site[h, pl.ds(p * chi + k * quarter, quarter), :] = block[p * quarter:(p + 1) * quarter, h * HALF:(h + 1) * HALF]
            return carry
        lax.fori_loop(0, d, load, 0, unroll=UNROLL)

    def reorder(parity):
        lp_copies[parity].wait()
        for k in range(2):
            part = mm(lp_ref[parity, :, k * wide:(k + 1) * wide], spread).astype(jnp.bfloat16)
            for s in range(d):
                lp_perm[parity, :, s * chi + k * HALF:s * chi + (k + 1) * HALF] = part[:, s * HALF:(s + 1) * HALF]

    def theta_gate(h, parity, lhs_ref, rhs_ref):
        def tile(at, carry):
            lhs = jnp.concatenate([
                jnp.concatenate([lhs_ref[q, pl.ds(u * chi + at * quarter, quarter), :] for q in range(2)], axis=1)
                for u in range(d)], axis=0)
            rhs = jnp.concatenate([rhs_ref[h, v * chi:(v + 1) * chi, :] for v in range(d)], axis=1)
            th = mm(lhs, rhs).astype(jnp.bfloat16)
            for pair in range(quarter // GROUP // 2):
                stack = jnp.concatenate([
                    jnp.concatenate([
                        th[u * quarter + (2 * pair + j) * GROUP:u * quarter + (2 * pair + j + 1) * GROUP, v * HALF:(v + 1) * HALF]
                        for v in range(d) for u in range(d)], axis=0)
                    for j in range(2)], axis=1)
                mixed = mm(w_ref[parity], stack)
                mixed = (mixed[:chi] + mixed[chi:]).astype(jnp.bfloat16)
                for j in range(2):
                    for t in range(d):
                        for s in range(d):
                            top = (t * d + s) * GROUP
                            gated[h, pl.ds(s * chi + at * quarter + (2 * pair + j) * GROUP, GROUP), t * HALF:(t + 1) * HALF] = (
                                mixed[top:top + GROUP, j * HALF:(j + 1) * HALF])
            return carry
        lax.fori_loop(0, d, tile, 0, unroll=UNROLL)

    def note(value):
        folded = value.reshape(value.shape[0] // 8, 8, value.shape[1])
        sq = jnp.sum(folded * folded, axis=0)
        mx = jnp.max(jnp.abs(folded), axis=0)
        for c in range(value.shape[1] // HALF):
            acc[0] += sq[:, c * HALF:(c + 1) * HALF]
            acc[1] = jnp.maximum(acc[1], mx[:, c * HALF:(c + 1) * HALF])

    def new_right(h, parity, dst, scale):
        value = mm(lp_perm[parity], gated[h])
        if scale is not None:
            value = value * scale
        note(value)
        value = value.astype(jnp.bfloat16)
        for t in range(d):
            dst[h, t * chi:(t + 1) * chi, :] = value[:, t * HALF:(t + 1) * HALF]

    def new_left(parity, dst, scale):
        def tile(s, carry):
            here = pl.ds(s * chi, chi)
            lhs = jnp.concatenate([gated[0, here, :], gated[1, here, :]], axis=1)
            rhs = jnp.concatenate([rp_ref[parity, t * chi + h * HALF:t * chi + (h + 1) * HALF, :]
                                   for h in range(2) for t in range(d)], axis=0)
            value = mm(lhs, rhs)
            if scale is not None:
                value = value * scale
            note(value)
            value = value.astype(jnp.bfloat16)
            for h in range(2):
                dst[h, here, :] = value[:, h * HALF:(h + 1) * HALF]
            return carry
        lax.fori_loop(0, d, tile, 0, unroll=UNROLL)

    def forward(k, h):
        return pltpu.make_async_remote_copy(
            src_ref=ahead.at[k, h], dst_ref=r_in.at[k, h], send_sem=fs.at[k, h], recv_sem=fr.at[k, h],
            device_id={"blk": left}, device_id_type=pl.DeviceIdType.MESH)

    def backward(k, h):
        return pltpu.make_async_remote_copy(
            src_ref=back.at[k, h], dst_ref=a_in.at[k, h], send_sem=bs.at[k, h], recv_sem=br.at[k, h],
            device_id={"blk": right}, device_id_type=pl.DeviceIdType.MESH)

    def everyone(layer):
        return pltpu.make_async_remote_copy(
            src_ref=seen.at[layer], dst_ref=seen.at[layer], send_sem=ss.at[layer], recv_sem=sr.at[layer],
            device_id={"blk": right}, device_id_type=pl.DeviceIdType.MESH)

    def share(layer):
        mine[layer, 0:1, :] = jnp.sum(acc[0], axis=0, keepdims=True)
        mine[layer, 1:2, :] = jnp.max(acc[1], axis=0, keepdims=True)

        def send(k, carry):
            pltpu.make_async_remote_copy(
                src_ref=mine.at[layer], dst_ref=seen.at[layer, k - 1], send_sem=ss.at[layer], recv_sem=sr.at[layer],
                device_id={"blk": lax.rem(me + k, n)}, device_id_type=pl.DeviceIdType.MESH).start()
            return carry
        lax.fori_loop(1, n, send, 0)
        acc[...] = jnp.zeros_like(acc)

    def learn(layer):
        everyone(layer).wait_recv()
        got = seen[layer]
        own = mine[layer]
        squares = jnp.sum(jnp.sum(got, axis=0)[0:1] + own[0:1], axis=1, keepdims=True)
        largest = jnp.max(jnp.maximum(jnp.max(got, axis=0)[1:2], own[1:2]), axis=1, keepdims=True)
        power = squares / entries + 1e-06
        root = jnp.sqrt(power)
        lane = lax.broadcasted_iota(jnp.int32, (1, 2), 1)
        rec_ref[layer:layer + 1, :] = jnp.where(lane == 0, jnp.log(root), jnp.log(largest / root))
        return power, root

    acc[...] = jnp.zeros_like(acc)
    scale, root = None, None
    for layer in range(LAYERS):
        parity, k = layer % 2, layer // 2
        if parity == 0:
            lhs = site_a
            if k > 0:
                lhs = a_in.at[k - 1]
                for h in range(2):
                    backward(k - 1, h).wait_recv()
            for h in range(2):
                theta_gate(h, parity, lhs, site_b)
            if layer > 0:
                power, root = learn(layer - 1)
                scale = 1.0 / power
            if layer == 0:
                rp_copies[0].wait()
            new_left(parity, ahead.at[k], scale)
            if layer == 0:
                pl.semaphore_wait(barrier, n - 1)
            for h in range(2):
                forward(k, h).start()
            if layer == 0:
                reorder(0)
            for h in range(2):
                new_right(h, parity, site_b, scale)
        else:
            for h in range(2):
                forward(k, h).wait_recv()
                theta_gate(h, parity, site_b, r_in.at[k])
                if h == 0:
                    power, root = learn(layer - 1)
                    scale = 1.0 / power
                new_right(h, parity, back.at[k], scale)
                backward(k, h).start()
            new_left(parity, site_b, scale)
        share(layer)
        if layer == 0:
            mixer(1)
            reorder(1)
            rp_copies[1].wait()

    last = LAYERS // 2 - 1
    for h in range(2):
        backward(last, h).wait_recv()
    power, root = learn(LAYERS - 1)
    shrink = 1.0 / root
    for which, site in ((0, a_in.at[last]), (1, site_b)):
        def store(kk, carry, which=which, site=site):
            block = jnp.concatenate([
                jnp.concatenate([site[h, pl.ds(p * chi + kk * quarter, quarter), :] for h in range(2)], axis=1)
                for p in range(d)], axis=0)
            out_ref[which, pl.ds(kk * quarter, quarter)] = (mm(to_plain, block) * shrink).astype(jnp.bfloat16).reshape(quarter, d, chi)
            return carry
        lax.fori_loop(0, d, store, 0, unroll=UNROLL)
    for k in range(LAYERS // 2):
        for h in range(2):
            forward(k, h).wait_send()
            backward(k, h).wait_send()
    for layer in range(LAYERS):
        everyone(layer).wait_send()


def local(tensors, gate_terms, right_proj, left_proj):
    slots, chi, d, _ = tensors.shape
    n = lax.axis_size("blk")
    entries = float(n * slots * chi * d * chi)
    vmem = pl.BlockSpec(memory_space=pltpu.VMEM)
    hbm = pl.BlockSpec(memory_space=pl.ANY)
    half = (2, d * chi, HALF)
    dma = pltpu.SemaphoreType.DMA
    pairs = LAYERS // 2
    evolved, records = pl.pallas_call(
        functools.partial(sweep_kernel, n, chi, d, entries),
        out_shape=(jax.ShapeDtypeStruct(tensors.shape, jnp.bfloat16),
                   jax.ShapeDtypeStruct((LAYERS, 2), jnp.float32)),
        in_specs=[hbm, vmem, hbm, hbm],
        out_specs=(vmem, vmem),
        scratch_shapes=[
            pltpu.VMEM(tensors.shape, jnp.bfloat16),
            pltpu.VMEM(right_proj.shape, jnp.bfloat16),
            pltpu.VMEM(left_proj.shape, jnp.bfloat16),
            pltpu.VMEM((2, 2 * d * d * GROUP, d * d * GROUP), jnp.bfloat16),
            pltpu.VMEM(half, jnp.bfloat16),
            pltpu.VMEM(half, jnp.bfloat16),
            pltpu.VMEM((pairs,) + half, jnp.bfloat16),
            pltpu.VMEM((pairs,) + half, jnp.bfloat16),
            pltpu.VMEM((pairs,) + half, jnp.bfloat16),
            pltpu.VMEM((pairs,) + half, jnp.bfloat16),
            pltpu.VMEM((2, d * chi, d * HALF), jnp.bfloat16),
            pltpu.VMEM((2, chi, d * chi), jnp.bfloat16),
            pltpu.VMEM((2, 8, HALF), jnp.float32),
            pltpu.VMEM((LAYERS, 2, HALF), jnp.float32),
            pltpu.VMEM((LAYERS, n - 1, 2, HALF), jnp.float32),
            dma((2,)), dma((2, 2)), dma((pairs, 2)), dma((pairs, 2)), dma((pairs, 2)), dma((pairs, 2)),
            dma((LAYERS,)), dma((LAYERS,)),
        ],
        compiler_params=pltpu.CompilerParams(collective_id=0, has_side_effects=True,
                                             vmem_limit_bytes=56 * 1024 * 1024),
        name="sweep",
    )(tensors, gate_terms, right_proj, left_proj)
    return evolved, records


def solution(mesh):
    in_specs = (
        P(("group", "blk"), None, None, None),
        P(),
        P("blk", None, None),
        P("blk", None, None),
    )
    out_specs = (P(("group", "blk"), None, None, None), P("group", None))
    return jax.shard_map(local, mesh=mesh, in_specs=in_specs, out_specs=out_specs, check_vma=False)
```

```python
import functools
import jax
import jax.numpy as jnp
from jax import lax
from jax.experimental import pallas as pl
from jax.experimental.pallas import tpu as pltpu
from jax.sharding import PartitionSpec as P

LAYERS = 4
HALF = 128
GROUP = 16
UNROLL = 4


def mm(a, b):
    return jnp.dot(a, b, preferred_element_type=jnp.float32)


def sweep_kernel(n, chi, d, entries, x_hbm, gate_ref, rp_hbm, lp_hbm, out_ref, rec_ref,
                 x_ref, rp_ref, lp_ref, w_ref, site_a, site_b, ahead, back, r_in, a_in, gated, lp_perm, acc, mine, seen,
                 xs, ps, fs, fr, bs, br, ss, sr):
    me = lax.axis_index("blk")
    right, left = lax.rem(me + 1, n), lax.rem(me + n - 1, n)
    quarter = chi // d
    barrier = pltpu.get_barrier_semaphore()
    x_copies = [pltpu.make_async_copy(x_hbm.at[i], x_ref.at[i], xs.at[i]) for i in range(2)]
    rp_copies = [pltpu.make_async_copy(rp_hbm.at[i], rp_ref.at[i], ps.at[0, i]) for i in range(2)]
    lp_copies = [pltpu.make_async_copy(lp_hbm.at[i], lp_ref.at[i], ps.at[1, i]) for i in range(2)]
    for copy in x_copies + [rp_copies[0], lp_copies[0], lp_copies[1], rp_copies[1]]:
        copy.start()

    def greet(k, carry):
        pl.semaphore_signal(barrier, inc=1, device_id={"blk": lax.rem(me + k, n)},
                            device_id_type=pl.DeviceIdType.MESH)
        return carry

    lax.fori_loop(1, n, greet, 0)

    rows = lax.broadcasted_iota(jnp.int32, (chi, chi), 0)
    cols = lax.broadcasted_iota(jnp.int32, (chi, chi), 1)
    to_block = jnp.where((rows // quarter == cols % d) & (rows % quarter == cols // d), 1.0, 0.0).astype(jnp.bfloat16)
    to_plain = jnp.where((cols // quarter == rows % d) & (cols % quarter == rows // d), 1.0, 0.0).astype(jnp.bfloat16)
    wide = d * HALF
    wrow = lax.broadcasted_iota(jnp.int32, (wide, wide), 0)
    wcol = lax.broadcasted_iota(jnp.int32, (wide, wide), 1)
    spread = jnp.where((wcol // HALF == wrow % d) & (wcol % HALF == wrow // d), 1.0, 0.0).astype(jnp.bfloat16)

    pairs = d * d
    pick_row = lax.broadcasted_iota(jnp.int32, (chi, pairs), 0) // GROUP
    pick_from = lax.broadcasted_iota(jnp.int32, (chi, pairs), 1)
    pick_left = jnp.where(pick_from == (pick_row % d) * d + pick_row // d, 1.0, 0.0).astype(jnp.bfloat16)
    pick_col = lax.broadcasted_iota(jnp.int32, (pairs, chi), 1) // GROUP
    pick_into = lax.broadcasted_iota(jnp.int32, (pairs, chi), 0)
    pick_right = jnp.where(pick_into == (pick_col % d) * d + pick_col // d, 1.0, 0.0).astype(jnp.bfloat16)
    same = rows % GROUP == cols % GROUP
    unit = jnp.where(lax.broadcasted_iota(jnp.int32, (pairs, pairs), 0)
                     == lax.broadcasted_iota(jnp.int32, (pairs, pairs), 1), 1.0, 0.0)

    def mixer(parity):
        table = unit + gate_ref[parity]
        high = table.astype(jnp.bfloat16)
        low = (table - high.astype(jnp.float32)).astype(jnp.bfloat16)
        for position, term in ((0, high), (1, low)):
            spread_rows = mm(pick_left, term).astype(jnp.bfloat16)
            full = jnp.where(same, mm(spread_rows, pick_right), 0.0)
            w_ref[parity, position * chi:(position + 1) * chi, :] = full.astype(jnp.bfloat16)

    mixer(0)

    for which, site in ((0, site_a), (1, site_b)):
        x_copies[which].wait()

        def load(k, carry, which=which, site=site):
            block = mm(to_block, x_ref[which, pl.ds(k * quarter, quarter)].reshape(chi, chi)).astype(jnp.bfloat16)
            for p in range(d):
                for h in range(2):
                    site[h, pl.ds(p * chi + k * quarter, quarter), :] = block[p * quarter:(p + 1) * quarter, h * HALF:(h + 1) * HALF]
            return carry
        lax.fori_loop(0, d, load, 0, unroll=UNROLL)

    def reorder(parity):
        lp_copies[parity].wait()
        for k in range(2):
            part = mm(lp_ref[parity, :, k * wide:(k + 1) * wide], spread).astype(jnp.bfloat16)
            for s in range(d):
                lp_perm[parity, :, s * chi + k * HALF:s * chi + (k + 1) * HALF] = part[:, s * HALF:(s + 1) * HALF]

    def theta_gate(h, parity, lhs_ref, rhs_ref):
        def tile(at, carry):
            lhs = jnp.concatenate([
                jnp.concatenate([lhs_ref[q, pl.ds(u * chi + at * quarter, quarter), :] for q in range(2)], axis=1)
                for u in range(d)], axis=0)
            rhs = jnp.concatenate([rhs_ref[h, v * chi:(v + 1) * chi, :] for v in range(d)], axis=1)
            th = mm(lhs, rhs).astype(jnp.bfloat16)
            for pair in range(quarter // GROUP // 2):
                stack = jnp.concatenate([
                    jnp.concatenate([
                        th[u * quarter + (2 * pair + j) * GROUP:u * quarter + (2 * pair + j + 1) * GROUP, v * HALF:(v + 1) * HALF]
                        for v in range(d) for u in range(d)], axis=0)
                    for j in range(2)], axis=1)
                mixed = mm(w_ref[parity], stack)
                mixed = (mixed[:chi] + mixed[chi:]).astype(jnp.bfloat16)
                for j in range(2):
                    for t in range(d):
                        for s in range(d):
                            top = (t * d + s) * GROUP
                            gated[h, pl.ds(s * chi + at * quarter + (2 * pair + j) * GROUP, GROUP), t * HALF:(t + 1) * HALF] = (
                                mixed[top:top + GROUP, j * HALF:(j + 1) * HALF])
            return carry
        lax.fori_loop(0, d, tile, 0, unroll=UNROLL)

    def note(value):
        folded = value.reshape(value.shape[0] // 8, 8, value.shape[1])
        sq = jnp.sum(folded * folded, axis=0)
        mx = jnp.max(jnp.abs(folded), axis=0)
        for c in range(value.shape[1] // HALF):
            acc[0] += sq[:, c * HALF:(c + 1) * HALF]
            acc[1] = jnp.maximum(acc[1], mx[:, c * HALF:(c + 1) * HALF])

    def new_right(h, parity, dst, scale):
        value = mm(lp_perm[parity], gated[h])
        if scale is not None:
            value = value * scale
        note(value)
        value = value.astype(jnp.bfloat16)
        for t in range(d):
            dst[h, t * chi:(t + 1) * chi, :] = value[:, t * HALF:(t + 1) * HALF]

    def piece(k, h, s):
        here = pl.ds(s * chi, chi)
        return pltpu.make_async_remote_copy(
            src_ref=ahead.at[k, h, here], dst_ref=r_in.at[k, h, here], send_sem=fs.at[k, h], recv_sem=fr.at[k, h],
            device_id={"blk": left}, device_id_type=pl.DeviceIdType.MESH)

    def new_left(parity, dst, scale, early=None):
        def tile(s, carry):
            here = pl.ds(s * chi, chi)
            lhs = jnp.concatenate([gated[0, here, :], gated[1, here, :]], axis=1)
            rhs = jnp.concatenate([rp_ref[parity, t * chi + h * HALF:t * chi + (h + 1) * HALF, :]
                                   for h in range(2) for t in range(d)], axis=0)
            value = mm(lhs, rhs)
            if scale is not None:
                value = value * scale
            note(value)
            value = value.astype(jnp.bfloat16)
            for h in range(2):
                dst[h, here, :] = value[:, h * HALF:(h + 1) * HALF]
            if early is not None:
                piece(early, 0, s).start()
            return carry
        lax.fori_loop(0, d, tile, 0, unroll=UNROLL)

    def forward(k, h):
        return pltpu.make_async_remote_copy(
            src_ref=ahead.at[k, h], dst_ref=r_in.at[k, h], send_sem=fs.at[k, h], recv_sem=fr.at[k, h],
            device_id={"blk": left}, device_id_type=pl.DeviceIdType.MESH)

    def backward(k, h):
        return pltpu.make_async_remote_copy(
            src_ref=back.at[k, h], dst_ref=a_in.at[k, h], send_sem=bs.at[k, h], recv_sem=br.at[k, h],
            device_id={"blk": right}, device_id_type=pl.DeviceIdType.MESH)

    def everyone(layer):
        return pltpu.make_async_remote_copy(
            src_ref=seen.at[layer], dst_ref=seen.at[layer], send_sem=ss.at[layer], recv_sem=sr.at[layer],
            device_id={"blk": right}, device_id_type=pl.DeviceIdType.MESH)

    def share(layer):
        mine[layer, 0:1, :] = jnp.sum(acc[0], axis=0, keepdims=True)
        mine[layer, 1:2, :] = jnp.max(acc[1], axis=0, keepdims=True)

        def send(k, carry):
            pltpu.make_async_remote_copy(
                src_ref=mine.at[layer], dst_ref=seen.at[layer, k - 1], send_sem=ss.at[layer], recv_sem=sr.at[layer],
                device_id={"blk": lax.rem(me + k, n)}, device_id_type=pl.DeviceIdType.MESH).start()
            return carry
        lax.fori_loop(1, n, send, 0)
        acc[...] = jnp.zeros_like(acc)

    def learn(layer):
        everyone(layer).wait_recv()
        got = seen[layer]
        own = mine[layer]
        squares = jnp.sum(jnp.sum(got, axis=0)[0:1] + own[0:1], axis=1, keepdims=True)
        largest = jnp.max(jnp.maximum(jnp.max(got, axis=0)[1:2], own[1:2]), axis=1, keepdims=True)
        power = squares / entries + 1e-06
        root = jnp.sqrt(power)
        lane = lax.broadcasted_iota(jnp.int32, (1, 2), 1)
        rec_ref[layer:layer + 1, :] = jnp.where(lane == 0, jnp.log(root), jnp.log(largest / root))
        return power, root

    acc[...] = jnp.zeros_like(acc)
    scale, root = None, None
    for layer in range(LAYERS):
        parity, k = layer % 2, layer // 2
        if parity == 0:
            lhs = site_a
            if k > 0:
                lhs = a_in.at[k - 1]
                for h in range(2):
                    backward(k - 1, h).wait_recv()
            for h in range(2):
                theta_gate(h, parity, lhs, site_b)
            if layer > 0:
                power, root = learn(layer - 1)
                scale = 1.0 / power
            if layer == 0:
                rp_copies[0].wait()
            new_left(parity, ahead.at[k], scale, k if k > 0 else None)
            if layer == 0:
                pl.semaphore_wait(barrier, n - 1)
            for h in range(1 if k > 0 else 0, 2):
                forward(k, h).start()
            if layer == 0:
                reorder(0)
            for h in range(2):
                new_right(h, parity, site_b, scale)
        else:
            for h in range(2):
                forward(k, h).wait_recv()
                theta_gate(h, parity, site_b, r_in.at[k])
                if h == 0:
                    power, root = learn(layer - 1)
                    scale = 1.0 / power
                new_right(h, parity, back.at[k], scale)
                backward(k, h).start()
            new_left(parity, site_b, scale)
        share(layer)
        if layer == 0:
            mixer(1)
            reorder(1)
            rp_copies[1].wait()

    last = LAYERS // 2 - 1
    for h in range(2):
        backward(last, h).wait_recv()
    power, root = learn(LAYERS - 1)
    shrink = 1.0 / root
    for which, site in ((0, a_in.at[last]), (1, site_b)):
        def store(kk, carry, which=which, site=site):
            block = jnp.concatenate([
                jnp.concatenate([site[h, pl.ds(p * chi + kk * quarter, quarter), :] for h in range(2)], axis=1)
                for p in range(d)], axis=0)
            out_ref[which, pl.ds(kk * quarter, quarter)] = (mm(to_plain, block) * shrink).astype(jnp.bfloat16).reshape(quarter, d, chi)
            return carry
        lax.fori_loop(0, d, store, 0, unroll=UNROLL)
    for k in range(LAYERS // 2):
        for h in range(2):
            forward(k, h).wait_send()
            backward(k, h).wait_send()
    for layer in range(LAYERS):
        everyone(layer).wait_send()


def local(tensors, gate_terms, right_proj, left_proj):
    slots, chi, d, _ = tensors.shape
    n = lax.axis_size("blk")
    entries = float(n * slots * chi * d * chi)
    vmem = pl.BlockSpec(memory_space=pltpu.VMEM)
    hbm = pl.BlockSpec(memory_space=pl.ANY)
    half = (2, d * chi, HALF)
    dma = pltpu.SemaphoreType.DMA
    pairs = LAYERS // 2
    evolved, records = pl.pallas_call(
        functools.partial(sweep_kernel, n, chi, d, entries),
        out_shape=(jax.ShapeDtypeStruct(tensors.shape, jnp.bfloat16),
                   jax.ShapeDtypeStruct((LAYERS, 2), jnp.float32)),
        in_specs=[hbm, vmem, hbm, hbm],
        out_specs=(vmem, vmem),
        scratch_shapes=[
            pltpu.VMEM(tensors.shape, jnp.bfloat16),
            pltpu.VMEM(right_proj.shape, jnp.bfloat16),
            pltpu.VMEM(left_proj.shape, jnp.bfloat16),
            pltpu.VMEM((2, 2 * d * d * GROUP, d * d * GROUP), jnp.bfloat16),
            pltpu.VMEM(half, jnp.bfloat16),
            pltpu.VMEM(half, jnp.bfloat16),
            pltpu.VMEM((pairs,) + half, jnp.bfloat16),
            pltpu.VMEM((pairs,) + half, jnp.bfloat16),
            pltpu.VMEM((pairs,) + half, jnp.bfloat16),
            pltpu.VMEM((pairs,) + half, jnp.bfloat16),
            pltpu.VMEM((2, d * chi, d * HALF), jnp.bfloat16),
            pltpu.VMEM((2, chi, d * chi), jnp.bfloat16),
            pltpu.VMEM((2, 8, HALF), jnp.float32),
            pltpu.VMEM((LAYERS, 2, HALF), jnp.float32),
            pltpu.VMEM((LAYERS, n - 1, 2, HALF), jnp.float32),
            dma((2,)), dma((2, 2)), dma((pairs, 2)), dma((pairs, 2)), dma((pairs, 2)), dma((pairs, 2)),
            dma((LAYERS,)), dma((LAYERS,)),
        ],
        compiler_params=pltpu.CompilerParams(collective_id=0, has_side_effects=True,
                                             vmem_limit_bytes=56 * 1024 * 1024),
        name="sweep",
    )(tensors, gate_terms, right_proj, left_proj)
    return evolved, records


def solution(mesh):
    in_specs = (
        P(("group", "blk"), None, None, None),
        P(),
        P("blk", None, None),
        P("blk", None, None),
    )
    out_specs = (P(("group", "blk"), None, None, None), P("group", None))
    return jax.shard_map(local, mesh=mesh, in_specs=in_specs, out_specs=out_specs, check_vma=False)
```
